32 devices in a mesh: groups: 2 (over y), cand: 8 (over z, x), tensor: 2 (over core).
Axes of the slice: x: 2, y: 2, z: 4, core: 2. Of those that a mesh axis runs over, the one named last changes fastest.
Arguments:
- queries: bfloat16 [4096, 512], P(('groups', 'cand'), 'tensor'), parts along dimension 0, may hold values from -8 to 8
- span_kv: bfloat16 [2, 4096, 128], P(None, ('groups', 'cand')), parts along dimension 1, may hold values from -10 to 10
- prefix_kv: bfloat16 [2, 2048, 128], P(None, ('groups', 'cand')), parts along dimension 1, may hold values from -8 to 8
- row_candidate: int32 [4096], P(('groups', 'cand')), parts along dimension 0, may hold values from -1 to 2047, as said below
- prefix_length: int32 [2], P('groups'), parts along dimension 0, may hold values from 512 to 1024
- out_weight: bfloat16 [512, 5120], P(None, 'tensor'), may hold values from -6 to 6
Outputs:
- attn_out: bfloat16 [4096, 5120], P(('groups', 'cand'), 'tensor'), parts along dimension 0
The draws below stay inside these ranges and needn't reach their ends.
There are 2 independent parts, one for each index of `groups`. The reference program is written for one: setup_inputs(seed, part) draws one part's arguments, and reference() takes and returns one part's arrays. A program takes and returns all parts, laid end to end along the dimension named above; an argument that names none is the same for every part. Nothing has to cross between parts.
Inputs may be any that keep to these rules, and one draw needn't show every extreme that they name: `row_candidate`: -1 marks an empty slot. On each index of cand the live slots come first and number 256 // 4 or more, and on some index all 256 slots are live. A candidate's slots are consecutive slots of one index of cand, and no other index uses its number.
All inputs are finite; a program needn't handle non-finite values.
Results may differ from the reference program's by a relative error of at most 0.0055.
Values may be sent and summed in bfloat16 or wider, within the bound.
A program may use at most 64 MiB of HBM per device.

```python
import math
import jax
import jax.numpy as jnp
from jax import lax

D = 5120
HD = 128
QHEADS = 4
CAP = 256
PREFIX = 1024
ROWS = 2048
N_CAND = 8


def draw_queries(key, part):
    draw_key = jax.random.fold_in(key, 21)
    base = jnp.clip(2.0 * jax.random.normal(draw_key, (ROWS, QHEADS * HD), jnp.float32), -8.0, 8.0)
    return base.astype(jnp.bfloat16)


def draw_prefix_kv(key, part):
    key_draw = jax.random.fold_in(key, 31)
    value_draw = jax.random.fold_in(key, 32)
    key_rows = jnp.clip(jax.random.normal(key_draw, (PREFIX, HD), jnp.float32), -8.0, 8.0)
    value_rows = jnp.clip(jax.random.normal(value_draw, (PREFIX, HD), jnp.float32), -8.0, 8.0)
    return jnp.stack([key_rows, value_rows]).astype(jnp.bfloat16)


def draw_row_candidate(key, part):
    holders = ROWS // CAP
    live_key = jax.random.fold_in(key, 41)
    full_key = jax.random.fold_in(key, 42)
    start_key = jax.random.fold_in(key, 43)
    live_counts = jax.random.randint(live_key, (holders,), CAP // 4, CAP + 1)
    full_holder = jax.random.randint(full_key, (), 0, holders)
    live_counts = live_counts.at[full_holder].set(CAP)
    starts = (jax.random.randint(start_key, (holders, CAP), 0, 96) == 0).astype(jnp.int32)
    starts = starts.at[:, 0].set(1)
    segment = jnp.cumsum(starts, axis=1) - 1
    numbers = jnp.arange(holders, dtype=jnp.int32)[:, None] * CAP + segment
    slots = jnp.arange(CAP, dtype=jnp.int32)[None, :]
    numbers = jnp.where(slots < live_counts[:, None], numbers, -1)
    return numbers.reshape(ROWS).astype(jnp.int32)


def shard_levels(rng, extent, shards, smallest, high):
    factor_of = 1.0
    for axis_at, blocks in shards:
        steps = jax.random.uniform(jax.random.fold_in(jax.random.fold_in(rng, 6), axis_at), (blocks,), jnp.float32, smallest / len(shards), high / len(shards))
        factor_of = factor_of * jnp.repeat(jnp.exp(steps), extent[axis_at] // blocks).reshape((-1,) + (1,) * (len(extent) - 1 - axis_at))
    return factor_of


def normal_values(key, shape, scale, limit, split=(), held_as=jnp.bfloat16):
    values = scale * jax.random.normal(key, shape, jnp.float32)
    if split:
        values = values * shard_levels(key, shape, split, -0.22, 0.18)
    return jnp.clip(values, -limit, limit).astype(held_as)


def setup_inputs(seed: int = 0, part: int = 0) -> dict:
    arg_keys = jax.random.split(jax.random.key(seed), 7)
    part_keys = jax.random.split(jax.random.fold_in(arg_keys[6], part), 7)
    queries = draw_queries(jax.random.fold_in(jax.random.fold_in(arg_keys[6], part), 71), part)
    span_kv = normal_values(part_keys[1], (2, ROWS, HD), 1.8, 10.0, ((1, 8),))
    prefix_kv = draw_prefix_kv(jax.random.fold_in(jax.random.fold_in(arg_keys[6], part), 71), part)
    row_candidate = draw_row_candidate(jax.random.fold_in(jax.random.fold_in(arg_keys[6], part), 71), part)
    prefix_length = jax.random.randint(part_keys[4], (1,), PREFIX // 2, PREFIX + 1).astype(jnp.int32)
    out_weight = normal_values(arg_keys[5], (QHEADS * HD, D), 1.0, 6.0, ((1, 2),))
    return dict(queries=queries, span_kv=span_kv, prefix_kv=prefix_kv, row_candidate=row_candidate, prefix_length=prefix_length, out_weight=out_weight)


NEG_BIG = -1e+30

def reference(queries, span_kv, prefix_kv, row_candidate, prefix_length, out_weight):
    scaling = 1.0 / math.sqrt(HD)
    live_length = prefix_length[0]
    prefix_keys = prefix_kv[0].astype(jnp.float32)
    prefix_values = prefix_kv[1].astype(jnp.float32)
    prefix_live = jnp.arange(PREFIX, dtype=jnp.int32) < live_length
    query_blocks = queries.reshape(N_CAND, CAP, QHEADS, HD)
    span_keys = span_kv[0].reshape(N_CAND, CAP, HD)
    span_values = span_kv[1].reshape(N_CAND, CAP, HD)
    candidates = row_candidate.reshape(N_CAND, CAP)
    positions = jnp.arange(CAP, dtype=jnp.int32)

    def one_device(inputs):
        query_rows, key_rows, value_rows, owners = inputs
        all_keys = jnp.concatenate([prefix_keys, key_rows.astype(jnp.float32)], axis=0)
        all_values = jnp.concatenate([prefix_values, value_rows.astype(jnp.float32)], axis=0)
        own = (owners[:, None] == owners[None, :]) & (positions[None, :] <= positions[:, None])
        allowed = jnp.concatenate([jnp.broadcast_to(prefix_live[None, :], (CAP, PREFIX)), own], axis=1)
        scores = jnp.einsum('rhd,kd->rhk', query_rows.astype(jnp.float32), all_keys) * scaling
        scores = jnp.where(allowed[:, None, :], scores, NEG_BIG)
        largest = lax.optimization_barrier(jnp.max(scores, axis=2, keepdims=True))
        weights = jnp.where(allowed[:, None, :], jnp.exp(scores - largest), 0.0)
        totals = lax.optimization_barrier(jnp.sum(weights, axis=2))
        rounded = weights.astype(jnp.bfloat16).astype(jnp.float32)
        head_out = jnp.einsum('rhk,kd->rhd', rounded, all_values) / totals[:, :, None]
        head_out = head_out.astype(jnp.bfloat16).reshape(CAP, QHEADS * HD)
        projected = jnp.dot(head_out, out_weight, preferred_element_type=jnp.float32)
        return jnp.where((owners >= 0)[:, None], projected, 0.0).astype(jnp.bfloat16)
    result = lax.map(one_device, (query_blocks, span_keys, span_values, candidates))
    return result.reshape(ROWS, D)
```

```python
import functools
import math

import jax
import jax.numpy as jnp
from jax import lax
from jax.experimental import pallas as pl
from jax.experimental.pallas import tpu as pltpu
from jax.sharding import PartitionSpec as P

HD = 128


NEG_BIG = -1e30


def swapped(block, axis, distance):
    count = lax.axis_size(axis)
    route = []
    for low in range(count):
        high = low | 1 << distance
        if high != low and high < count:
            route += [(low, high), (high, low)]
    return lax.ppermute(block, axis, route)


def attend(running, query_rows, key_rows, value_rows, allowed):
    maxima, totals, weighted = running
    scores = lax.dot_general(
        query_rows, key_rows, (((1,), (1,)), ((), ())), preferred_element_type=jnp.float32
    )
    scores = scores * (1.0 / math.sqrt(HD))
    scores = jnp.where(allowed, scores, NEG_BIG)
    newest = jnp.maximum(maxima, jnp.max(scores, axis=1))
    shrink = jnp.exp(maxima - newest)
    weights = jnp.where(allowed, jnp.exp(scores - newest[:, None]), 0.0)
    totals = totals * shrink + jnp.sum(weights, axis=1)
    weighted = weighted * shrink[:, None] + jnp.dot(
        weights.astype(jnp.bfloat16), value_rows, preferred_element_type=jnp.float32
    )
    return (newest, totals, weighted)


def prefix_fold(running, pieces, offset, query_rows, live_length):
    key_rows, value_rows = pieces
    length = key_rows.shape[0]
    width = math.gcd(length, 2048)
    rounds = length // width
    key_blocks = key_rows.reshape(rounds, width, key_rows.shape[1])
    value_blocks = value_rows.reshape(rounds, width, value_rows.shape[1])
    firsts = jnp.arange(rounds, dtype=jnp.int32) * width

    def visit(carried, inputs):
        keys_here, values_here, first = inputs
        places = offset + first + lax.iota(jnp.int32, width)
        allowed = (places < live_length)[None, :]
        return (attend(carried, query_rows, keys_here, values_here, allowed), None)

    running, unused = lax.scan(visit, running, (key_blocks, value_blocks, firsts))
    return running


def body_large(queries, span_kv, prefix_kv, row_candidate, prefix_length, out_weight):
    slots = queries.shape[0]
    head_size = span_kv.shape[2]
    heads_here = queries.shape[1] // head_size
    query_rows = queries.reshape(slots * heads_here, head_size)
    live_length = prefix_length[0]
    stacked = slots * heads_here
    initial = (
        jnp.full((stacked,), NEG_BIG, jnp.float32),
        jnp.zeros((stacked,), jnp.float32),
        jnp.zeros((stacked, head_size), jnp.float32),
    )
    positions = lax.iota(jnp.int32, slots)
    own = (row_candidate[:, None] == row_candidate[None, :]) & (
        positions[None, :] <= positions[:, None]
    )
    own = jnp.repeat(own, heads_here, axis=0)
    core_index = lax.axis_index("tensor")
    mine = jnp.where(core_index == 0, prefix_kv[0], prefix_kv[1])
    gathered = lax.all_gather(mine, "cand", axis=0, tiled=True)
    partner = swapped(gathered, "tensor", 0)
    key_rows = jnp.where(core_index == 0, gathered, partner)
    value_rows = jnp.where(core_index == 0, partner, gathered)
    result = prefix_fold(initial, (key_rows, value_rows), 0, query_rows, live_length)
    running = result
    running = attend(running, query_rows, span_kv[0], span_kv[1], own)
    maxima, totals, weighted = running
    head_out = (
        (weighted / totals[:, None]).astype(jnp.bfloat16).reshape(slots, heads_here * head_size)
    )
    both_heads = lax.all_gather(head_out, "tensor", axis=1, tiled=True)
    projected = jnp.dot(both_heads, out_weight, preferred_element_type=jnp.float32)
    return jnp.where((row_candidate >= 0)[:, None], projected, 0.0).astype(jnp.bfloat16)


MESH = pl.DeviceIdType.MESH

EARLY = ((), (0,), (0,), (0, 1), (0,), (0, 1), (0,), (0, 1))
LATE = ((1, 2, 4, 6), (3, 5, 7), (3, 6, 4), (2, 7, 5), (5, 2, 6), (4, 3, 7), (7, 2, 4), (6, 3, 5))
FORWARD = ((2, 4, 6), (), (0, 4, 6), (1, 5, 7), (0, 2, 6), (1, 3, 7), (0, 2, 4), (1, 3, 5))
ORDER = (
    (1, 2, 3, 4, 6, 5, 7),
    (3, 5, 0, 7, 2, 4, 6),
    (3, 0, 4, 6, 1, 5, 7),
    (2, 1, 5, 7, 0, 4, 6),
    (5, 6, 2, 0, 7, 3, 1),
    (4, 7, 3, 1, 6, 2, 0),
    (7, 4, 2, 0, 5, 3, 1),
    (6, 5, 3, 1, 4, 2, 0),
)


def gather_attend(
    n,
    q_hbm,
    span_hbm,
    prefix_hbm,
    rows_hbm,
    weight_hbm,
    length_hbm,
    head_ref,
    weight_ref,
    q_buf,
    span_buf,
    own_buf,
    rows_buf,
    length_ref,
    kv_buf,
    bias_buf,
    m_buf,
    l_buf,
    acc_buf,
    local_sem,
    q_sem,
    send_sem,
    forward_sem,
    recv_sem,
    relay_send_sem,
    relay_recv_sem,
):
    me = lax.axis_index("cand")
    core = lax.axis_index("tensor")
    other = 1 - core
    slots, width = q_hbm.shape
    depth, head_size = prefix_hbm.shape[1:]
    heads_here = width // head_size
    factor = math.log2(math.e) / math.sqrt(head_size)
    barrier = pltpu.get_barrier_semaphore()
    late_receivers = [sorted({*LATE[c], *([c ^ 1] if FORWARD[c] else [])}) for c in range(n)]

    def greet(cand, tensor):
        pl.semaphore_signal(
            barrier, inc=1, device_id={"cand": cand, "tensor": tensor}, device_id_type=MESH
        )

    def on(tensor, c):
        return pl.when((core == tensor) & (me == c))

    def remote(src, dst, send, recv, device_id):
        return pltpu.make_async_remote_copy(
            src_ref=src,
            dst_ref=dst,
            send_sem=send,
            recv_sem=recv,
            device_id=device_id,
            device_id_type=MESH,
        )

    def own_send(src, c, to):
        at = ORDER[to].index(c)
        return remote(
            src, kv_buf.at[at], send_sem.at[to], recv_sem.at[at], {"cand": to, "tensor": 1}
        )

    def forward(c, source):
        at, there = ORDER[c].index(source), ORDER[c ^ 1].index(source)
        return remote(
            kv_buf.at[at],
            kv_buf.at[there],
            forward_sem.at[at],
            recv_sem.at[there],
            {"cand": c ^ 1, "tensor": 1},
        )

    def relay(at):
        return remote(
            kv_buf.at[at],
            kv_buf.at[at],
            relay_send_sem.at[at],
            relay_recv_sem.at[at],
            {"tensor": other},
        )

    for c in range(n):

        @on(1, c)
        def _(c=c):
            for sender in range(n):
                if c in EARLY[sender]:
                    greet(sender, 0)
            for sender in range(n):
                if c in late_receivers[sender]:
                    greet(sender, 1)

    @pl.when(core == 1)
    def _():
        greet(me, 0)

    loads = [
        pltpu.make_async_copy(rows_hbm, rows_buf, local_sem.at[0]),
        pltpu.make_async_copy(q_hbm, q_buf.at[core], local_sem.at[1]),
        pltpu.make_async_copy(span_hbm, span_buf, local_sem.at[2]),
        pltpu.make_async_copy(prefix_hbm, own_buf, local_sem.at[3]),
        pltpu.make_async_copy(length_hbm, length_ref, local_sem.at[5]),
    ]
    for load in loads:
        load.start()
    weight_load = pltpu.make_async_copy(weight_hbm, weight_ref, local_sem.at[4])

    q_send = remote(q_hbm, q_buf.at[core], q_sem.at[0], q_sem.at[1], {"tensor": other})
    q_in = remote(
        q_buf.at[other], q_buf.at[other], q_sem.at[0], q_sem.at[1], {"tensor": other}
    )

    def send_late(c, src):
        pl.semaphore_wait(barrier, len(late_receivers[c]))
        for to in LATE[c]:
            own_send(src, c, to).start()

    for c in range(n):

        @on(0, c)
        def _(c=c):
            pl.semaphore_wait(barrier, len(EARLY[c]) + 1)
            for to in EARLY[c]:
                own_send(prefix_hbm, c, to).start()

        if c >= n // 2:

            @on(1, c)
            def _(c=c):
                send_late(c, prefix_hbm)

    @pl.when(core == 0)
    def _():
        q_send.start()

    weight_load.start()

    def scores_of(side, j, key_rows):
        query_rows = q_buf[side, :, j * head_size : (j + 1) * head_size]
        return lax.dot_general(
            key_rows, query_rows, (((1,), (1,)), ((), ())), preferred_element_type=jnp.float32
        )

    def weighted(value_rows, weights):
        return lax.dot_general(
            value_rows,
            weights.astype(jnp.bfloat16),
            (((0,), (0,)), ((), ())),
            preferred_element_type=jnp.float32,
        )

    def start_with_span(side):
        for j in range(heads_here):
            scores = scores_of(side, j, span_buf[0]) + bias_buf[...]
            newest = jnp.max(scores, axis=0, keepdims=True)
            weights = jnp.exp2((scores - newest) * factor)
            m_buf[side, j] = newest
            l_buf[side, j] = jnp.sum(weights, axis=0, keepdims=True)
            acc_buf[side, j] = weighted(span_buf[1], weights)

    def fold(sides, pieces):
        keys, values, bias = [], [], []
        for ref, source in pieces:
            keys.append(ref[0])
            values.append(ref[1])
            at = source * depth + lax.broadcasted_iota(jnp.int32, (depth, slots), 0)
            bias.append(jnp.where(at < length_ref[0], 0.0, NEG_BIG))
        key_rows = keys[0] if len(keys) == 1 else jnp.concatenate(keys, axis=0)
        value_rows = values[0] if len(keys) == 1 else jnp.concatenate(values, axis=0)
        key_bias = bias[0] if len(keys) == 1 else jnp.concatenate(bias, axis=0)
        for side in sides:
            for j in range(heads_here):
                scores = scores_of(side, j, key_rows) + key_bias
                before = m_buf[side, j]
                newest = jnp.maximum(before, jnp.max(scores, axis=0, keepdims=True))
                shrink = jnp.exp2((before - newest) * factor)
                weights = jnp.exp2((scores - newest) * factor)
                m_buf[side, j] = newest
                l_buf[side, j] = l_buf[side, j] * shrink + jnp.sum(weights, axis=0, keepdims=True)
                acc_buf[side, j] = acc_buf[side, j] * shrink + weighted(value_rows, weights)

    loads[0].wait()
    across_rows = jnp.broadcast_to(rows_buf[...].reshape(1, slots), (slots, slots))
    down_rows = across_rows.T
    key_at = lax.broadcasted_iota(jnp.int32, (slots, slots), 0)
    row_at = lax.broadcasted_iota(jnp.int32, (slots, slots), 1)
    allowed = (across_rows == down_rows) & (key_at <= row_at)
    bias_buf[...] = jnp.where(allowed, 0.0, NEG_BIG)
    live_row = across_rows[:1] >= 0

    for load in loads[1:]:
        load.wait()
    start_with_span(core)
    fold((core,), [(own_buf, me)])
    q_in.wait_recv()

    @pl.when(core == 1)
    def _():
        q_send.start()

    start_with_span(other)
    fold((other,), [(own_buf, me)])

    for c in range(n // 2):

        @on(1, c)
        def _(c=c):
            send_late(c, own_buf)

    def arrive(at):
        @pl.when(core == 0)
        def _():
            relay(at).wait_recv()

        @pl.when(core == 1)
        def _():
            remote(
                kv_buf.at[at], kv_buf.at[at], send_sem.at[0], recv_sem.at[at], {"tensor": other}
            ).wait_recv()
            relay(at).start()
            for c in range(n):
                if ORDER[c][at] in FORWARD[c]:

                    @pl.when(me == c)
                    def _(c=c):
                        forward(c, ORDER[c][at]).start()

    def source_of(at):
        return sum((me == c).astype(jnp.int32) * ORDER[c][at] for c in range(n))

    for at in range(n - 1):
        arrive(at)
        fold((core, other), [(kv_buf.at[at], source_of(at))])

    for side in (core, other):
        for j in range(heads_here):
            out = jnp.where(live_row, acc_buf[side, j] * (1.0 / l_buf[side, j]), 0.0).T
            first = pl.multiple_of((side * heads_here + j) * head_size, head_size)
            head_ref[:, pl.ds(first, head_size)] = out.astype(head_ref.dtype)

    weight_load.wait()
    q_send.wait_send()
    for c in range(n):

        @on(0, c)
        def _(c=c):
            for to in EARLY[c]:
                own_send(prefix_hbm, c, to).wait_send()

        @on(1, c)
        def _(c=c):
            for to in LATE[c]:
                own_send(prefix_hbm, c, to).wait_send()
            for source in FORWARD[c]:
                forward(c, source).wait_send()

    @pl.when(core == 1)
    def _():
        for at in range(n - 1):
            relay(at).wait_send()


def project(head_ref, weight_ref, out_hbm, tiles, sems):
    copies = []
    block = tiles.shape[2]
    for at in range(tiles.shape[0]):
        columns = slice(at * block, (at + 1) * block)
        tiles[at] = jnp.dot(
            head_ref[...], weight_ref[:, columns], preferred_element_type=jnp.float32
        ).astype(tiles.dtype)
        copies.append(pltpu.make_async_copy(tiles.at[at], out_hbm.at[:, columns], sems.at[at]))
        copies[-1].start()
    for copy in copies:
        copy.wait()


def body(n, queries, span_kv, prefix_kv, row_candidate, prefix_length, out_weight):
    slots, width = queries.shape
    depth, head_size = prefix_kv.shape[1:]
    heads_here = width // head_size
    anywhere = pl.BlockSpec(memory_space=pltpu.HBM)
    operands = (queries, span_kv, prefix_kv, row_candidate, out_weight)
    row_state = pltpu.VMEM((2, heads_here, 1, slots), jnp.float32)
    both_heads, weight = pl.pallas_call(
        functools.partial(gather_attend, n),
        name="gather_attend",
        out_shape=(
            jax.ShapeDtypeStruct((slots, 2 * width), jnp.bfloat16),
            jax.ShapeDtypeStruct(out_weight.shape, jnp.bfloat16),
        ),
        in_specs=[anywhere] * len(operands) + [pl.BlockSpec(memory_space=pl.ANY)],
        out_specs=[pl.BlockSpec(memory_space=pltpu.VMEM)] * 2,
        scratch_shapes=[
            pltpu.VMEM((2, slots, width), jnp.bfloat16),
            pltpu.VMEM(span_kv.shape, jnp.bfloat16),
            pltpu.VMEM(prefix_kv.shape, jnp.bfloat16),
            pltpu.VMEM(row_candidate.shape, jnp.int32),
            pltpu.SMEM(prefix_length.shape, jnp.int32),
            pltpu.VMEM((n - 1, *prefix_kv.shape), jnp.bfloat16),
            pltpu.VMEM((slots, slots), jnp.float32),
            row_state,
            row_state,
            pltpu.VMEM((2, heads_here, head_size, slots), jnp.float32),
            pltpu.SemaphoreType.DMA((6,)),
            pltpu.SemaphoreType.DMA((2,)),
            pltpu.SemaphoreType.DMA((n,)),
            pltpu.SemaphoreType.DMA((n,)),
            pltpu.SemaphoreType.DMA((n,)),
            pltpu.SemaphoreType.DMA((n,)),
            pltpu.SemaphoreType.DMA((n,)),
        ],
        compiler_params=pltpu.CompilerParams(
            collective_id=0, has_side_effects=True, vmem_limit_bytes=24 << 20
        ),
    )(*[pltpu.with_memory_space_constraint(x, pltpu.HBM) for x in operands], prefix_length)
    features = out_weight.shape[1]
    block = math.gcd(features, 512)
    return pl.pallas_call(
        project,
        name="project",
        out_shape=jax.ShapeDtypeStruct((slots, features), jnp.bfloat16),
        in_specs=[pl.BlockSpec(memory_space=pltpu.VMEM)] * 2,
        out_specs=pl.BlockSpec(memory_space=pltpu.HBM),
        scratch_shapes=[
            pltpu.VMEM((features // block, slots, block), jnp.bfloat16),
            pltpu.SemaphoreType.DMA((features // block,)),
        ],
        compiler_params=pltpu.CompilerParams(vmem_limit_bytes=24 << 20),
    )(both_heads, weight)


def solution(mesh):
    n = mesh.shape["cand"]
    run = functools.partial(body, n) if n == 8 and mesh.shape["tensor"] == 2 else body_large
    return jax.shard_map(
        run,
        mesh=mesh,
        in_specs=(
            P(("groups", "cand"), "tensor"),
            P(None, ("groups", "cand"), None),
            P(None, ("groups", "cand"), None),
            P(("groups", "cand")),
            P("groups"),
            P(None, "tensor"),
        ),
        out_specs=P(("groups", "cand"), "tensor"),
        check_vma=False,
    )
```

```python
import functools
import math

import jax
import jax.numpy as jnp
from jax import lax
from jax.experimental import pallas as pl
from jax.experimental.pallas import tpu as pltpu
from jax.sharding import PartitionSpec as P

HD = 128


NEG_BIG = -1e30


def swapped(block, axis, distance):
    count = lax.axis_size(axis)
    route = []
    for low in range(count):
        high = low | 1 << distance
        if high != low and high < count:
            route += [(low, high), (high, low)]
    return lax.ppermute(block, axis, route)


def attend(running, query_rows, key_rows, value_rows, allowed):
    maxima, totals, weighted = running
    scores = lax.dot_general(
        query_rows, key_rows, (((1,), (1,)), ((), ())), preferred_element_type=jnp.float32
    )
    scores = scores * (1.0 / math.sqrt(HD))
    scores = jnp.where(allowed, scores, NEG_BIG)
    newest = jnp.maximum(maxima, jnp.max(scores, axis=1))
    shrink = jnp.exp(maxima - newest)
    weights = jnp.where(allowed, jnp.exp(scores - newest[:, None]), 0.0)
    totals = totals * shrink + jnp.sum(weights, axis=1)
    weighted = weighted * shrink[:, None] + jnp.dot(
        weights.astype(jnp.bfloat16), value_rows, preferred_element_type=jnp.float32
    )
    return (newest, totals, weighted)


def prefix_fold(running, pieces, offset, query_rows, live_length):
    key_rows, value_rows = pieces
    length = key_rows.shape[0]
    width = math.gcd(length, 2048)
    rounds = length // width
    key_blocks = key_rows.reshape(rounds, width, key_rows.shape[1])
    value_blocks = value_rows.reshape(rounds, width, value_rows.shape[1])
    firsts = jnp.arange(rounds, dtype=jnp.int32) * width

    def visit(carried, inputs):
        keys_here, values_here, first = inputs
        places = offset + first + lax.iota(jnp.int32, width)
        allowed = (places < live_length)[None, :]
        return (attend(carried, query_rows, keys_here, values_here, allowed), None)

    running, unused = lax.scan(visit, running, (key_blocks, value_blocks, firsts))
    return running


def body_large(queries, span_kv, prefix_kv, row_candidate, prefix_length, out_weight):
    slots = queries.shape[0]
    head_size = span_kv.shape[2]
    heads_here = queries.shape[1] // head_size
    query_rows = queries.reshape(slots * heads_here, head_size)
    live_length = prefix_length[0]
    stacked = slots * heads_here
    initial = (
        jnp.full((stacked,), NEG_BIG, jnp.float32),
        jnp.zeros((stacked,), jnp.float32),
        jnp.zeros((stacked, head_size), jnp.float32),
    )
    positions = lax.iota(jnp.int32, slots)
    own = (row_candidate[:, None] == row_candidate[None, :]) & (
        positions[None, :] <= positions[:, None]
    )
    own = jnp.repeat(own, heads_here, axis=0)
    core_index = lax.axis_index("tensor")
    mine = jnp.where(core_index == 0, prefix_kv[0], prefix_kv[1])
    gathered = lax.all_gather(mine, "cand", axis=0, tiled=True)
    partner = swapped(gathered, "tensor", 0)
    key_rows = jnp.where(core_index == 0, gathered, partner)
    value_rows = jnp.where(core_index == 0, partner, gathered)
    result = prefix_fold(initial, (key_rows, value_rows), 0, query_rows, live_length)
    running = result
    running = attend(running, query_rows, span_kv[0], span_kv[1], own)
    maxima, totals, weighted = running
    head_out = (
        (weighted / totals[:, None]).astype(jnp.bfloat16).reshape(slots, heads_here * head_size)
    )
    both_heads = lax.all_gather(head_out, "tensor", axis=1, tiled=True)
    projected = jnp.dot(both_heads, out_weight, preferred_element_type=jnp.float32)
    return jnp.where((row_candidate >= 0)[:, None], projected, 0.0).astype(jnp.bfloat16)


MESH = pl.DeviceIdType.MESH

EARLY = ((2, ), (6, 7, ), (0, ), (4, 2, ), (0, ), (6, 0, 4, ), (2, 1, 5, 7, 4, ), (3, 4, 5, 6, ), )
LATE = ((7, 1, 4, 5, 6, ), (0, 5, 3, 2, ), (6, 5, 3, 1, ), (0, 7, 6, ), (3, 5, 6, ), (7, 1, 2, 3, ), (0, ), (1, 0, ), )
FORWARD = ((4, 3, ), (), (6, 0, ), (7, 4, ), (3, ), (2, 1, ), (2, 4, ), (), )
ORDER = ((4, 1, 2, 6, 3, 7, 5, ), (7, 2, 4, 0, 6, 3, 5, ), (0, 6, 1, 3, 4, 7, 5, ), (4, 7, 1, 0, 6, 5, 2, ), (3, 5, 0, 7, 2, 1, 6, ), (2, 1, 4, 3, 0, 7, 6, ), (4, 2, 7, 3, 0, 1, 5, ), (4, 3, 5, 6, 0, 1, 2, ), )
PRE = (1, 2, 3, 4, 6, 7)

def gather_attend(
    n,
    q_hbm,
    span_hbm,
    prefix_hbm,
    rows_hbm,
    weight_hbm,
    length_hbm,
    head_ref,
    weight_ref,
    q_buf,
    span_buf,
    own_buf,
    rows_buf,
    length_ref,
    kv_buf,
    bias_buf,
    m_buf,
    l_buf,
    acc_buf,
    local_sem,
    q_sem,
    send_sem,
    forward_sem,
    recv_sem,
    relay_send_sem,
    relay_recv_sem,
):
    me = lax.axis_index("cand")
    core = lax.axis_index("tensor")
    other = 1 - core
    slots, width = q_hbm.shape
    depth, head_size = prefix_hbm.shape[1:]
    heads_here = width // head_size
    factor = math.log2(math.e) / math.sqrt(head_size)
    barrier = pltpu.get_barrier_semaphore()
    late_receivers = [sorted({*LATE[c], *([c ^ 1] if FORWARD[c] else [])}) for c in range(n)]

    def greet(cand, tensor):
        pl.semaphore_signal(
            barrier, inc=1, device_id={"cand": cand, "tensor": tensor}, device_id_type=MESH
        )

    def on(tensor, c):
        return pl.when((core == tensor) & (me == c))

    def remote(src, dst, send, recv, device_id):
        return pltpu.make_async_remote_copy(
            src_ref=src,
            dst_ref=dst,
            send_sem=send,
            recv_sem=recv,
            device_id=device_id,
            device_id_type=MESH,
        )

    def own_send(src, c, to):
        at = ORDER[to].index(c)
        return remote(
            src,
            kv_buf.at[at],
            send_sem.at[0],
            recv_sem.at[at],
            {"cand": to, "tensor": 1},
        )

    def forward(c, source):
        at, there = ORDER[c].index(source), ORDER[c ^ 1].index(source)
        return remote(
            kv_buf.at[at],
            kv_buf.at[there],
            forward_sem.at[0],
            recv_sem.at[there],
            {"cand": c ^ 1, "tensor": 1},
        )

    def relay(at):
        return remote(
            kv_buf.at[at],
            kv_buf.at[at],
            relay_send_sem.at[0],
            relay_recv_sem.at[at],
            {"tensor": other},
        )

    def arrival(at):
        return remote(
            kv_buf.at[at],
            kv_buf.at[at],
            send_sem.at[0],
            recv_sem.at[at],
            {"tensor": other},
        )

    for c in range(n):

        @on(1, c)
        def _(c=c):
            for sender in range(n):
                if c in EARLY[sender]:
                    greet(sender, 0)
            for sender in range(n):
                if c in late_receivers[sender]:
                    greet(sender, 1)

    @pl.when(core == 1)
    def _():
        greet(me, 0)

    loads = [
        pltpu.make_async_copy(rows_hbm, rows_buf, local_sem.at[0]),
        pltpu.make_async_copy(q_hbm, q_buf.at[0], local_sem.at[1]),
        pltpu.make_async_copy(span_hbm, span_buf, local_sem.at[2]),
        pltpu.make_async_copy(prefix_hbm, own_buf, local_sem.at[3]),
        pltpu.make_async_copy(length_hbm, length_ref, local_sem.at[5]),
    ]
    for load in loads:
        load.start()
    weight_load = pltpu.make_async_copy(weight_hbm, weight_ref, local_sem.at[4])

    q_send = remote(q_hbm, q_buf.at[1], q_sem.at[0], q_sem.at[1], {"tensor": other})

    def send_late(c, src):
        pl.semaphore_wait(barrier, len(late_receivers[c]))
        for to in LATE[c]:
            own_send(src, c, to).start()

    for c in range(n):

        @on(0, c)
        def _(c=c):
            pl.semaphore_wait(barrier, len(EARLY[c]) + 1)
            for to in EARLY[c]:
                own_send(prefix_hbm, c, to).start()

        if c in PRE:

            @on(1, c)
            def _(c=c):
                send_late(c, prefix_hbm)

    @pl.when(core == 0)
    def _():
        q_send.start()

    weight_load.start()

    def scores_of(side, j, key_rows):
        query_rows = q_buf[side, :, j * head_size : (j + 1) * head_size]
        return lax.dot_general(
            key_rows, query_rows, (((1,), (1,)), ((), ())), preferred_element_type=jnp.float32
        )

    def weighted(value_rows, weights):
        return lax.dot_general(
            value_rows,
            weights.astype(jnp.bfloat16),
            (((0,), (0,)), ((), ())),
            preferred_element_type=jnp.float32,
        )

    def start_with_span(side):
        for j in range(heads_here):
            scores = scores_of(side, j, span_buf[0]) + bias_buf[...]
            newest = jnp.max(scores, axis=0, keepdims=True)
            weights = jnp.exp2((scores - newest) * factor)
            m_buf[side, j] = newest
            l_buf[side, j] = jnp.sum(weights, axis=0, keepdims=True)
            acc_buf[side, j] = weighted(span_buf[1], weights)

    def fold(sides, pieces):
        keys, values, bias = [], [], []
        for ref, source in pieces:
            keys.append(ref[0])
            values.append(ref[1])
            at = source * depth + lax.broadcasted_iota(jnp.int32, (depth, slots), 0)
            bias.append(jnp.where(at < length_ref[0], 0.0, NEG_BIG))
        key_rows = keys[0] if len(keys) == 1 else jnp.concatenate(keys, axis=0)
        value_rows = values[0] if len(keys) == 1 else jnp.concatenate(values, axis=0)
        key_bias = bias[0] if len(keys) == 1 else jnp.concatenate(bias, axis=0)
        for side in sides:
            for j in range(heads_here):
                scores = scores_of(side, j, key_rows) + key_bias
                before = m_buf[side, j]
                newest = jnp.maximum(before, jnp.max(scores, axis=0, keepdims=True))
                shrink = jnp.exp2((before - newest) * factor)
                weights = jnp.exp2((scores - newest) * factor)
                m_buf[side, j] = newest
                l_buf[side, j] = l_buf[side, j] * shrink + jnp.sum(weights, axis=0, keepdims=True)
                acc_buf[side, j] = acc_buf[side, j] * shrink + weighted(value_rows, weights)

    loads[0].wait()
    across_rows = jnp.broadcast_to(rows_buf[...].reshape(1, slots), (slots, slots))
    down_rows = across_rows.T
    key_at = lax.broadcasted_iota(jnp.int32, (slots, slots), 0)
    row_at = lax.broadcasted_iota(jnp.int32, (slots, slots), 1)
    allowed = (across_rows == down_rows) & (key_at <= row_at)
    bias_buf[...] = jnp.where(allowed, 0.0, NEG_BIG)
    live_row = across_rows[:1] >= 0

    for load in loads[1:]:
        load.wait()
    start_with_span(0)
    fold((0,), [(own_buf, me)])
    q_send.wait_recv()

    @pl.when(core == 1)
    def _():
        q_send.start()

    start_with_span(1)
    fold((1,), [(own_buf, me)])

    for c in range(n):
        if c not in PRE:

            @on(1, c)
            def _(c=c):
                send_late(c, own_buf)

    def arrive(at):
        @pl.when(core == 0)
        def _():
            relay(at).wait_recv()

        @pl.when(core == 1)
        def _():
            arrival(at).wait_recv()
            relay(at).start()
            for c in range(n):
                if ORDER[c][at] in FORWARD[c]:

                    @pl.when(me == c)
                    def _(c=c):
                        forward(c, ORDER[c][at]).start()

    def sent(blocks, sem):
        part = kv_buf.at[pl.ds(0, blocks)]
        remote(part, part, sem.at[0], recv_sem.at[0], {"tensor": other}).wait_send()

    def source_of(at):
        return sum((me == c).astype(jnp.int32) * ORDER[c][at] for c in range(n))

    for at in range(n - 1):
        if at == n - 2:
            weight_load.wait()
            q_send.wait_send()
            for c in range(n):
                if EARLY[c]:

                    @on(0, c)
                    def _(c=c):
                        sent(len(EARLY[c]), send_sem)

                if LATE[c]:

                    @on(1, c)
                    def _(c=c):
                        sent(len(LATE[c]), send_sem)

        arrive(at)
        fold((0, 1), [(kv_buf.at[at], source_of(at))])

    for side in (0, 1):
        for j in range(heads_here):
            out = jnp.where(live_row, acc_buf[side, j] * (1.0 / l_buf[side, j]), 0.0).T
            place = (core if side == 0 else other) * heads_here + j
            first = pl.multiple_of(place * head_size, head_size)
            head_ref[:, pl.ds(first, head_size)] = out.astype(head_ref.dtype)

    @pl.when(core == 1)
    def _():
        sent(n - 1, relay_send_sem)
        for c in range(n):
            if FORWARD[c]:

                @pl.when(me == c)
                def _(c=c):
                    sent(len(FORWARD[c]), forward_sem)


def project(head_ref, weight_ref, out_hbm, tiles, sems):
    copies = []
    block = tiles.shape[2]
    for at in range(tiles.shape[0]):
        columns = slice(at * block, (at + 1) * block)
        tiles[at] = jnp.dot(
            head_ref[...], weight_ref[:, columns], preferred_element_type=jnp.float32
        ).astype(tiles.dtype)
        copies.append(pltpu.make_async_copy(tiles.at[at], out_hbm.at[:, columns], sems.at[at]))
        copies[-1].start()
    for copy in copies:
        copy.wait()


def body(n, queries, span_kv, prefix_kv, row_candidate, prefix_length, out_weight):
    slots, width = queries.shape
    depth, head_size = prefix_kv.shape[1:]
    heads_here = width // head_size
    anywhere = pl.BlockSpec(memory_space=pltpu.HBM)
    operands = (queries, span_kv, prefix_kv, row_candidate, out_weight)
    row_state = pltpu.VMEM((2, heads_here, 1, slots), jnp.float32)
    both_heads, weight = pl.pallas_call(
        functools.partial(gather_attend, n),
        name="gather_attend",
        out_shape=(
            jax.ShapeDtypeStruct((slots, 2 * width), jnp.bfloat16),
            jax.ShapeDtypeStruct(out_weight.shape, jnp.bfloat16),
        ),
        in_specs=[anywhere] * len(operands) + [pl.BlockSpec(memory_space=pl.ANY)],
        out_specs=[pl.BlockSpec(memory_space=pltpu.VMEM)] * 2,
        scratch_shapes=[
            pltpu.VMEM((2, slots, width), jnp.bfloat16),
            pltpu.VMEM(span_kv.shape, jnp.bfloat16),
            pltpu.VMEM(prefix_kv.shape, jnp.bfloat16),
            pltpu.VMEM(row_candidate.shape, jnp.int32),
            pltpu.SMEM(prefix_length.shape, jnp.int32),
            pltpu.VMEM((n - 1, *prefix_kv.shape), jnp.bfloat16),
            pltpu.VMEM((slots, slots), jnp.float32),
            row_state,
            row_state,
            pltpu.VMEM((2, heads_here, head_size, slots), jnp.float32),
            pltpu.SemaphoreType.DMA((6,)),
            pltpu.SemaphoreType.DMA((2,)),
            pltpu.SemaphoreType.DMA((1,)),
            pltpu.SemaphoreType.DMA((1,)),
            pltpu.SemaphoreType.DMA((n,)),
            pltpu.SemaphoreType.DMA((1,)),
            pltpu.SemaphoreType.DMA((n,)),
        ],
        compiler_params=pltpu.CompilerParams(
            collective_id=0, has_side_effects=True, vmem_limit_bytes=24 << 20
        ),
    )(*[pltpu.with_memory_space_constraint(x, pltpu.HBM) for x in operands], prefix_length)
    features = out_weight.shape[1]
    block = math.gcd(features, 512)
    return pl.pallas_call(
        project,
        name="project",
        out_shape=jax.ShapeDtypeStruct((slots, features), jnp.bfloat16),
        in_specs=[pl.BlockSpec(memory_space=pltpu.VMEM)] * 2,
        out_specs=pl.BlockSpec(memory_space=pltpu.HBM),
        scratch_shapes=[
            pltpu.VMEM((features // block, slots, block), jnp.bfloat16),
            pltpu.SemaphoreType.DMA((features // block,)),
        ],
        compiler_params=pltpu.CompilerParams(vmem_limit_bytes=24 << 20),
    )(both_heads, weight)


def solution(mesh):
    n = mesh.shape["cand"]
    run = functools.partial(body, n) if n == 8 and mesh.shape["tensor"] == 2 else body_large
    return jax.shard_map(
        run,
        mesh=mesh,
        in_specs=(
            P(("groups", "cand"), "tensor"),
            P(None, ("groups", "cand"), None),
            P(None, ("groups", "cand"), None),
            P(("groups", "cand")),
            P("groups"),
            P(None, "tensor"),
        ),
        out_specs=P(("groups", "cand"), "tensor"),
        check_vma=False,
    )
```

```python
import functools
import math

import jax
import jax.numpy as jnp
from jax import lax
from jax.experimental import pallas as pl
from jax.experimental.pallas import tpu as pltpu
from jax.sharding import PartitionSpec as P

HD = 128


NEG_BIG = -1e30


def swapped(block, axis, distance):
    count = lax.axis_size(axis)
    route = []
    for low in range(count):
        high = low | 1 << distance
        if high != low and high < count:
            route += [(low, high), (high, low)]
    return lax.ppermute(block, axis, route)


def attend(running, query_rows, key_rows, value_rows, allowed):
    maxima, totals, weighted = running
    scores = lax.dot_general(
        query_rows, key_rows, (((1,), (1,)), ((), ())), preferred_element_type=jnp.float32
    )
    scores = scores * (1.0 / math.sqrt(HD))
    scores = jnp.where(allowed, scores, NEG_BIG)
    newest = jnp.maximum(maxima, jnp.max(scores, axis=1))
    shrink = jnp.exp(maxima - newest)
    weights = jnp.where(allowed, jnp.exp(scores - newest[:, None]), 0.0)
    totals = totals * shrink + jnp.sum(weights, axis=1)
    weighted = weighted * shrink[:, None] + jnp.dot(
        weights.astype(jnp.bfloat16), value_rows, preferred_element_type=jnp.float32
    )
    return (newest, totals, weighted)


def prefix_fold(running, pieces, offset, query_rows, live_length):
    key_rows, value_rows = pieces
    length = key_rows.shape[0]
    width = math.gcd(length, 2048)
    rounds = length // width
    key_blocks = key_rows.reshape(rounds, width, key_rows.shape[1])
    value_blocks = value_rows.reshape(rounds, width, value_rows.shape[1])
    firsts = jnp.arange(rounds, dtype=jnp.int32) * width

    def visit(carried, inputs):
        keys_here, values_here, first = inputs
        places = offset + first + lax.iota(jnp.int32, width)
        allowed = (places < live_length)[None, :]
        return (attend(carried, query_rows, keys_here, values_here, allowed), None)

    running, unused = lax.scan(visit, running, (key_blocks, value_blocks, firsts))
    return running


def body_large(queries, span_kv, prefix_kv, row_candidate, prefix_length, out_weight):
    slots = queries.shape[0]
    head_size = span_kv.shape[2]
    heads_here = queries.shape[1] // head_size
    query_rows = queries.reshape(slots * heads_here, head_size)
    live_length = prefix_length[0]
    stacked = slots * heads_here
    initial = (
        jnp.full((stacked,), NEG_BIG, jnp.float32),
        jnp.zeros((stacked,), jnp.float32),
        jnp.zeros((stacked, head_size), jnp.float32),
    )
    positions = lax.iota(jnp.int32, slots)
    own = (row_candidate[:, None] == row_candidate[None, :]) & (
        positions[None, :] <= positions[:, None]
    )
    own = jnp.repeat(own, heads_here, axis=0)
    core_index = lax.axis_index("tensor")
    mine = jnp.where(core_index == 0, prefix_kv[0], prefix_kv[1])
    gathered = lax.all_gather(mine, "cand", axis=0, tiled=True)
    partner = swapped(gathered, "tensor", 0)
    key_rows = jnp.where(core_index == 0, gathered, partner)
    value_rows = jnp.where(core_index == 0, partner, gathered)
    result = prefix_fold(initial, (key_rows, value_rows), 0, query_rows, live_length)
    running = result
    running = attend(running, query_rows, span_kv[0], span_kv[1], own)
    maxima, totals, weighted = running
    head_out = (
        (weighted / totals[:, None]).astype(jnp.bfloat16).reshape(slots, heads_here * head_size)
    )
    both_heads = lax.all_gather(head_out, "tensor", axis=1, tiled=True)
    projected = jnp.dot(both_heads, out_weight, preferred_element_type=jnp.float32)
    return jnp.where((row_candidate >= 0)[:, None], projected, 0.0).astype(jnp.bfloat16)


MESH = pl.DeviceIdType.MESH

EARLY = ((2, ), (6, 7, ), (0, ), (4, 2, ), (0, ), (0, 6, 4, ), (2, 1, 5, 7, 4, ), (3, 4, 5, 6, ), )
LATE = ((7, 1, 4, 5, 6, ), (0, 5, 3, 2, ), (6, 5, 3, 1, ), (0, 7, 6, ), (3, 5, 6, ), (7, 1, 2, 3, ), (0, ), (1, 0, ), )
FORWARD = ((4, 3, ), (), (6, 0, ), (7, 4, ), (3, ), (2, 1, ), (2, 4, ), (), )
ORDER = ((4, 1, 2, 6, 3, 7, 5, ), (7, 0, 2, 4, 6, 5, 3, ), (0, 6, 1, 3, 4, 7, 5, ), (4, 2, 7, 1, 0, 6, 5, ), (3, 5, 0, 7, 2, 1, 6, ), (2, 1, 4, 3, 0, 7, 6, ), (4, 2, 0, 7, 3, 5, 1, ), (4, 3, 5, 6, 0, 1, 2, ), )
PRE = (1, 2, 3, 4, 6, 7)

def gather_attend(
    n,
    q_hbm,
    span_hbm,
    prefix_hbm,
    rows_hbm,
    weight_hbm,
    length_hbm,
    head_ref,
    weight_ref,
    q_buf,
    span_buf,
    own_buf,
    rows_buf,
    length_ref,
    kv_buf,
    bias_buf,
    m_buf,
    l_buf,
    acc_buf,
    local_sem,
    q_sem,
    send_sem,
    forward_sem,
    recv_sem,
    relay_send_sem,
    relay_recv_sem,
):
    me = lax.axis_index("cand")
    core = lax.axis_index("tensor")
    other = 1 - core
    slots, width = q_hbm.shape
    depth, head_size = prefix_hbm.shape[1:]
    heads_here = width // head_size
    factor = math.log2(math.e) / math.sqrt(head_size)
    barrier = pltpu.get_barrier_semaphore()
    late_receivers = [sorted({*LATE[c], *([c ^ 1] if FORWARD[c] else [])}) for c in range(n)]

    def greet(cand, tensor):
        pl.semaphore_signal(
            barrier, inc=1, device_id={"cand": cand, "tensor": tensor}, device_id_type=MESH
        )

    def on(tensor, c):
        return pl.when((core == tensor) & (me == c))

    def remote(src, dst, send, recv, device_id):
        return pltpu.make_async_remote_copy(
            src_ref=src,
            dst_ref=dst,
            send_sem=send,
            recv_sem=recv,
            device_id=device_id,
            device_id_type=MESH,
        )

    def own_send(src, c, to):
        at = ORDER[to].index(c)
        return remote(
            src,
            kv_buf.at[at],
            send_sem.at[0],
            recv_sem.at[at],
            {"cand": to, "tensor": 1},
        )

    def forward(c, source):
        at, there = ORDER[c].index(source), ORDER[c ^ 1].index(source)
        return remote(
            kv_buf.at[at],
            kv_buf.at[there],
            forward_sem.at[0],
            recv_sem.at[there],
            {"cand": c ^ 1, "tensor": 1},
        )

    def relay(at):
        return remote(
            kv_buf.at[at],
            kv_buf.at[at],
            relay_send_sem.at[0],
            relay_recv_sem.at[at],
            {"tensor": other},
        )

    def arrival(at):
        return remote(
            kv_buf.at[at],
            kv_buf.at[at],
            send_sem.at[0],
            recv_sem.at[at],
            {"tensor": other},
        )

    for c in range(n):

        @on(1, c)
        def _(c=c):
            for sender in range(n):
                if c in EARLY[sender]:
                    greet(sender, 0)
            for sender in range(n):
                if c in late_receivers[sender]:
                    greet(sender, 1)

    @pl.when(core == 1)
    def _():
        greet(me, 0)

    loads = [
        pltpu.make_async_copy(rows_hbm, rows_buf, local_sem.at[0]),
        pltpu.make_async_copy(q_hbm, q_buf.at[0], local_sem.at[1]),
        pltpu.make_async_copy(span_hbm, span_buf, local_sem.at[2]),
        pltpu.make_async_copy(prefix_hbm, own_buf, local_sem.at[3]),
        pltpu.make_async_copy(length_hbm, length_ref, local_sem.at[5]),
    ]
    for load in loads:
        load.start()
    weight_load = pltpu.make_async_copy(weight_hbm, weight_ref, local_sem.at[4])

    q_send = remote(q_hbm, q_buf.at[1], q_sem.at[0], q_sem.at[1], {"tensor": other})

    def send_late(c, src):
        pl.semaphore_wait(barrier, len(late_receivers[c]))
        for to in LATE[c]:
            own_send(src, c, to).start()

    for c in range(n):

        @on(0, c)
        def _(c=c):
            pl.semaphore_wait(barrier, len(EARLY[c]) + 1)
            for to in EARLY[c]:
                own_send(prefix_hbm, c, to).start()

        if c in PRE:

            @on(1, c)
            def _(c=c):
                send_late(c, prefix_hbm)

    @pl.when(core == 0)
    def _():
        q_send.start()

    weight_load.start()

    def scores_of(side, j, key_rows):
        query_rows = q_buf[side, :, j * head_size : (j + 1) * head_size]
        return lax.dot_general(
            key_rows, query_rows, (((1,), (1,)), ((), ())), preferred_element_type=jnp.float32
        )

    def weighted(value_rows, weights):
        return lax.dot_general(
            value_rows,
            weights.astype(jnp.bfloat16),
            (((0,), (0,)), ((), ())),
            preferred_element_type=jnp.float32,
        )

    def start_with_span(side):
        for j in range(heads_here):
            scores = scores_of(side, j, span_buf[0]) + bias_buf[...]
            newest = jnp.max(scores, axis=0, keepdims=True)
            weights = jnp.exp2((scores - newest) * factor)
            m_buf[side, j] = newest
            l_buf[side, j] = jnp.sum(weights, axis=0, keepdims=True)
            acc_buf[side, j] = weighted(span_buf[1], weights)

    def fold(sides, pieces):
        keys, values, bias = [], [], []
        for ref, source in pieces:
            keys.append(ref[0])
            values.append(ref[1])
            at = source * depth + lax.broadcasted_iota(jnp.int32, (depth, slots), 0)
            bias.append(jnp.where(at < length_ref[0], 0.0, NEG_BIG))
        key_rows = keys[0] if len(keys) == 1 else jnp.concatenate(keys, axis=0)
        value_rows = values[0] if len(keys) == 1 else jnp.concatenate(values, axis=0)
        key_bias = bias[0] if len(keys) == 1 else jnp.concatenate(bias, axis=0)
        for side in sides:
            for j in range(heads_here):
                scores = scores_of(side, j, key_rows) + key_bias
                before = m_buf[side, j]
                newest = jnp.maximum(before, jnp.max(scores, axis=0, keepdims=True))
                shrink = jnp.exp2((before - newest) * factor)
                weights = jnp.exp2((scores - newest) * factor)
                m_buf[side, j] = newest
                l_buf[side, j] = l_buf[side, j] * shrink + jnp.sum(weights, axis=0, keepdims=True)
                acc_buf[side, j] = acc_buf[side, j] * shrink + weighted(value_rows, weights)

    loads[0].wait()
    across_rows = jnp.broadcast_to(rows_buf[...].reshape(1, slots), (slots, slots))
    down_rows = across_rows.T
    key_at = lax.broadcasted_iota(jnp.int32, (slots, slots), 0)
    row_at = lax.broadcasted_iota(jnp.int32, (slots, slots), 1)
    allowed = (across_rows == down_rows) & (key_at <= row_at)
    bias_buf[...] = jnp.where(allowed, 0.0, NEG_BIG)
    live_row = across_rows[:1] >= 0

    for load in loads[1:]:
        load.wait()
    start_with_span(0)
    fold((0,), [(own_buf, me)])
    q_send.wait_recv()

    @pl.when(core == 1)
    def _():
        q_send.start()

    start_with_span(1)
    fold((1,), [(own_buf, me)])

    for c in range(n):
        if c not in PRE:

            @on(1, c)
            def _(c=c):
                send_late(c, own_buf)

    def arrive(at):
        @pl.when(core == 0)
        def _():
            relay(at).wait_recv()

        @pl.when(core == 1)
        def _():
            arrival(at).wait_recv()
            relay(at).start()
            for c in range(n):
                if ORDER[c][at] in FORWARD[c]:

                    @pl.when(me == c)
                    def _(c=c):
                        forward(c, ORDER[c][at]).start()

    def sent(blocks, sem):
        part = kv_buf.at[pl.ds(0, blocks)]
        remote(part, part, sem.at[0], recv_sem.at[0], {"tensor": other}).wait_send()

    def source_of(at):
        return sum((me == c).astype(jnp.int32) * ORDER[c][at] for c in range(n))

    for at in range(n - 1):
        if at == n - 2:
            weight_load.wait()
            q_send.wait_send()
            for c in range(n):
                if EARLY[c]:

                    @on(0, c)
                    def _(c=c):
                        sent(len(EARLY[c]), send_sem)

                if LATE[c]:

                    @on(1, c)
                    def _(c=c):
                        sent(len(LATE[c]), send_sem)

        arrive(at)
        fold((0, 1), [(kv_buf.at[at], source_of(at))])

    for side in (0, 1):
        for j in range(heads_here):
            out = jnp.where(live_row, acc_buf[side, j] * (1.0 / l_buf[side, j]), 0.0).T
            place = (core if side == 0 else other) * heads_here + j
            first = pl.multiple_of(place * head_size, head_size)
            head_ref[:, pl.ds(first, head_size)] = out.astype(head_ref.dtype)

    @pl.when(core == 1)
    def _():
        sent(n - 1, relay_send_sem)
        for c in range(n):
            if FORWARD[c]:

                @pl.when(me == c)
                def _(c=c):
                    sent(len(FORWARD[c]), forward_sem)


def project(head_ref, weight_ref, out_hbm, tiles, sems):
    copies = []
    block = tiles.shape[2]
    for at in range(tiles.shape[0]):
        columns = slice(at * block, (at + 1) * block)
        tiles[at] = jnp.dot(
            head_ref[...], weight_ref[:, columns], preferred_element_type=jnp.float32
        ).astype(tiles.dtype)
        copies.append(pltpu.make_async_copy(tiles.at[at], out_hbm.at[:, columns], sems.at[at]))
        copies[-1].start()
    for copy in copies:
        copy.wait()


def body(n, queries, span_kv, prefix_kv, row_candidate, prefix_length, out_weight):
    slots, width = queries.shape
    depth, head_size = prefix_kv.shape[1:]
    heads_here = width // head_size
    anywhere = pl.BlockSpec(memory_space=pltpu.HBM)
    operands = (queries, span_kv, prefix_kv, row_candidate, out_weight)
    row_state = pltpu.VMEM((2, heads_here, 1, slots), jnp.float32)
    both_heads, weight = pl.pallas_call(
        functools.partial(gather_attend, n),
        name="gather_attend",
        out_shape=(
            jax.ShapeDtypeStruct((slots, 2 * width), jnp.bfloat16),
            jax.ShapeDtypeStruct(out_weight.shape, jnp.bfloat16),
        ),
        in_specs=[anywhere] * len(operands) + [pl.BlockSpec(memory_space=pl.ANY)],
        out_specs=[pl.BlockSpec(memory_space=pltpu.VMEM)] * 2,
        scratch_shapes=[
            pltpu.VMEM((2, slots, width), jnp.bfloat16),
            pltpu.VMEM(span_kv.shape, jnp.bfloat16),
            pltpu.VMEM(prefix_kv.shape, jnp.bfloat16),
            pltpu.VMEM(row_candidate.shape, jnp.int32),
            pltpu.SMEM(prefix_length.shape, jnp.int32),
            pltpu.VMEM((n - 1, *prefix_kv.shape), jnp.bfloat16),
            pltpu.VMEM((slots, slots), jnp.float32),
            row_state,
            row_state,
            pltpu.VMEM((2, heads_here, head_size, slots), jnp.float32),
            pltpu.SemaphoreType.DMA((6,)),
            pltpu.SemaphoreType.DMA((2,)),
            pltpu.SemaphoreType.DMA((1,)),
            pltpu.SemaphoreType.DMA((1,)),
            pltpu.SemaphoreType.DMA((n,)),
            pltpu.SemaphoreType.DMA((1,)),
            pltpu.SemaphoreType.DMA((n,)),
        ],
        compiler_params=pltpu.CompilerParams(
            collective_id=0, has_side_effects=True, vmem_limit_bytes=24 << 20
        ),
    )(*[pltpu.with_memory_space_constraint(x, pltpu.HBM) for x in operands], prefix_length)
    features = out_weight.shape[1]
    block = math.gcd(features, 512)
    return pl.pallas_call(
        project,
        name="project",
        out_shape=jax.ShapeDtypeStruct((slots, features), jnp.bfloat16),
        in_specs=[pl.BlockSpec(memory_space=pltpu.VMEM)] * 2,
        out_specs=pl.BlockSpec(memory_space=pltpu.HBM),
        scratch_shapes=[
            pltpu.VMEM((features // block, slots, block), jnp.bfloat16),
            pltpu.SemaphoreType.DMA((features // block,)),
        ],
        compiler_params=pltpu.CompilerParams(vmem_limit_bytes=24 << 20),
    )(both_heads, weight)


def solution(mesh):
    n = mesh.shape["cand"]
    run = functools.partial(body, n) if n == 8 and mesh.shape["tensor"] == 2 else body_large
    return jax.shard_map(
        run,
        mesh=mesh,
        in_specs=(
            P(("groups", "cand"), "tensor"),
            P(None, ("groups", "cand"), None),
            P(None, ("groups", "cand"), None),
            P(("groups", "cand")),
            P("groups"),
            P(None, "tensor"),
        ),
        out_specs=P(("groups", "cand"), "tensor"),
        check_vma=False,
    )
```

```python
import functools
import math

import jax
import jax.numpy as jnp
from jax import lax
from jax.experimental import pallas as pl
from jax.experimental.pallas import tpu as pltpu
from jax.sharding import PartitionSpec as P

HD = 128


NEG_BIG = -1e30


def swapped(block, axis, distance):
    count = lax.axis_size(axis)
    route = []
    for low in range(count):
        high = low | 1 << distance
        if high != low and high < count:
            route += [(low, high), (high, low)]
    return lax.ppermute(block, axis, route)


def attend(running, query_rows, key_rows, value_rows, allowed):
    maxima, totals, weighted = running
    scores = lax.dot_general(
        query_rows, key_rows, (((1,), (1,)), ((), ())), preferred_element_type=jnp.float32
    )
    scores = scores * (1.0 / math.sqrt(HD))
    scores = jnp.where(allowed, scores, NEG_BIG)
    newest = jnp.maximum(maxima, jnp.max(scores, axis=1))
    shrink = jnp.exp(maxima - newest)
    weights = jnp.where(allowed, jnp.exp(scores - newest[:, None]), 0.0)
    totals = totals * shrink + jnp.sum(weights, axis=1)
    weighted = weighted * shrink[:, None] + jnp.dot(
        weights.astype(jnp.bfloat16), value_rows, preferred_element_type=jnp.float32
    )
    return (newest, totals, weighted)


def prefix_fold(running, pieces, offset, query_rows, live_length):
    key_rows, value_rows = pieces
    length = key_rows.shape[0]
    width = math.gcd(length, 2048)
    rounds = length // width
    key_blocks = key_rows.reshape(rounds, width, key_rows.shape[1])
    value_blocks = value_rows.reshape(rounds, width, value_rows.shape[1])
    firsts = jnp.arange(rounds, dtype=jnp.int32) * width

    def visit(carried, inputs):
        keys_here, values_here, first = inputs
        places = offset + first + lax.iota(jnp.int32, width)
        allowed = (places < live_length)[None, :]
        return (attend(carried, query_rows, keys_here, values_here, allowed), None)

    running, unused = lax.scan(visit, running, (key_blocks, value_blocks, firsts))
    return running


def body_large(queries, span_kv, prefix_kv, row_candidate, prefix_length, out_weight):
    slots = queries.shape[0]
    head_size = span_kv.shape[2]
    heads_here = queries.shape[1] // head_size
    query_rows = queries.reshape(slots * heads_here, head_size)
    live_length = prefix_length[0]
    stacked = slots * heads_here
    initial = (
        jnp.full((stacked,), NEG_BIG, jnp.float32),
        jnp.zeros((stacked,), jnp.float32),
        jnp.zeros((stacked, head_size), jnp.float32),
    )
    positions = lax.iota(jnp.int32, slots)
    own = (row_candidate[:, None] == row_candidate[None, :]) & (
        positions[None, :] <= positions[:, None]
    )
    own = jnp.repeat(own, heads_here, axis=0)
    core_index = lax.axis_index("tensor")
    mine = jnp.where(core_index == 0, prefix_kv[0], prefix_kv[1])
    gathered = lax.all_gather(mine, "cand", axis=0, tiled=True)
    partner = swapped(gathered, "tensor", 0)
    key_rows = jnp.where(core_index == 0, gathered, partner)
    value_rows = jnp.where(core_index == 0, partner, gathered)
    result = prefix_fold(initial, (key_rows, value_rows), 0, query_rows, live_length)
    running = result
    running = attend(running, query_rows, span_kv[0], span_kv[1], own)
    maxima, totals, weighted = running
    head_out = (
        (weighted / totals[:, None]).astype(jnp.bfloat16).reshape(slots, heads_here * head_size)
    )
    both_heads = lax.all_gather(head_out, "tensor", axis=1, tiled=True)
    projected = jnp.dot(both_heads, out_weight, preferred_element_type=jnp.float32)
    return jnp.where((row_candidate >= 0)[:, None], projected, 0.0).astype(jnp.bfloat16)


MESH = pl.DeviceIdType.MESH

EARLY = ((2, ), (6, 7, ), (0, ), (4, 2, ), (0, ), (0, 6, 4, ), (2, 1, 5, 7, 4, ), (3, 4, 5, 6, ), )
LATE = ((7, 1, 4, 5, 6, ), (0, 5, 3, 2, ), (6, 5, 3, 1, ), (0, 7, 6, ), (3, 5, 6, ), (7, 1, 2, 3, ), (0, ), (1, 0, ), )
FORWARD = ((4, 3, ), (), (6, 0, ), (7, 4, ), (3, ), (2, 1, ), (2, 4, ), (), )
ORDER = ((4, 1, 2, 6, 3, 7, 5, ), (7, 0, 2, 4, 6, 5, 3, ), (0, 6, 1, 3, 4, 7, 5, ), (4, 2, 7, 1, 0, 6, 5, ), (3, 5, 0, 7, 2, 1, 6, ), (2, 1, 4, 3, 0, 7, 6, ), (4, 2, 0, 7, 3, 5, 1, ), (4, 3, 5, 6, 0, 1, 2, ), )
PRE = (1, 2, 3, 4, 6, 7)

def gather_attend(
    n,
    q_hbm,
    span_hbm,
    prefix_hbm,
    rows_hbm,
    weight_hbm,
    length_hbm,
    head_ref,
    weight_ref,
    q_buf,
    span_buf,
    own_buf,
    rows_buf,
    length_ref,
    kv_buf,
    bias_buf,
    m_buf,
    l_buf,
    acc_buf,
    local_sem,
    q_sem,
    send_sem,
    forward_sem,
    recv_sem,
    relay_send_sem,
    relay_recv_sem,
):
    me = lax.axis_index("cand")
    core = lax.axis_index("tensor")
    other = 1 - core
    slots, width = q_hbm.shape
    depth, head_size = prefix_hbm.shape[1:]
    heads_here = width // head_size
    factor = math.log2(math.e) / math.sqrt(head_size)
    barrier = pltpu.get_barrier_semaphore()
    late_receivers = [sorted({*LATE[c], *([c ^ 1] if FORWARD[c] else [])}) for c in range(n)]

    def greet(cand, tensor):
        pl.semaphore_signal(
            barrier, inc=1, device_id={"cand": cand, "tensor": tensor}, device_id_type=MESH
        )

    def on(tensor, c):
        return pl.when((core == tensor) & (me == c))

    def remote(src, dst, send, recv, device_id):
        return pltpu.make_async_remote_copy(
            src_ref=src,
            dst_ref=dst,
            send_sem=send,
            recv_sem=recv,
            device_id=device_id,
            device_id_type=MESH,
        )

    def own_send(src, c, to):
        at = ORDER[to].index(c)
        return remote(
            src,
            kv_buf.at[at],
            send_sem.at[0],
            recv_sem.at[at],
            {"cand": to, "tensor": 1},
        )

    def forward(c, source):
        at, there = ORDER[c].index(source), ORDER[c ^ 1].index(source)
        return remote(
            kv_buf.at[at],
            kv_buf.at[there],
            forward_sem.at[0],
            recv_sem.at[there],
            {"cand": c ^ 1, "tensor": 1},
        )

    def relay(at):
        return remote(
            kv_buf.at[at],
            kv_buf.at[at],
            relay_send_sem.at[0],
            relay_recv_sem.at[at],
            {"tensor": other},
        )

    def arrival(at):
        return remote(
            kv_buf.at[at],
            kv_buf.at[at],
            send_sem.at[0],
            recv_sem.at[at],
            {"tensor": other},
        )

    for c in range(n):

        @on(1, c)
        def _(c=c):
            for sender in range(n):
                if c in late_receivers[sender]:
                    greet(sender, 1)
            for sender in range(n):
                if c in EARLY[sender]:
                    greet(sender, 0)

    @pl.when(core == 1)
    def _():
        greet(me, 0)

    loads = [
        pltpu.make_async_copy(rows_hbm, rows_buf, local_sem.at[0]),
        pltpu.make_async_copy(q_hbm, q_buf.at[0], local_sem.at[1]),
        pltpu.make_async_copy(span_hbm, span_buf, local_sem.at[2]),
        pltpu.make_async_copy(prefix_hbm, own_buf, local_sem.at[3]),
        pltpu.make_async_copy(length_hbm, length_ref, local_sem.at[5]),
    ]
    for load in loads:
        load.start()
    weight_load = pltpu.make_async_copy(weight_hbm, weight_ref, local_sem.at[4])

    q_send = remote(q_hbm, q_buf.at[1], q_sem.at[0], q_sem.at[1], {"tensor": other})

    def send_late(c, src):
        pl.semaphore_wait(barrier, len(late_receivers[c]))
        for to in LATE[c]:
            own_send(src, c, to).start()

    for c in range(n):

        @on(0, c)
        def _(c=c):
            pl.semaphore_wait(barrier, len(EARLY[c]) + 1)
            for to in EARLY[c]:
                own_send(prefix_hbm, c, to).start()

        if c in PRE:

            @on(1, c)
            def _(c=c):
                send_late(c, prefix_hbm)

    @pl.when(core == 0)
    def _():
        q_send.start()


    def scores_of(side, j, key_rows):
        query_rows = q_buf[side, :, j * head_size : (j + 1) * head_size]
        return lax.dot_general(
            key_rows, query_rows, (((1,), (1,)), ((), ())), preferred_element_type=jnp.float32
        )

    def weighted(value_rows, weights):
        return lax.dot_general(
            value_rows,
            weights.astype(jnp.bfloat16),
            (((0,), (0,)), ((), ())),
            preferred_element_type=jnp.float32,
        )

    def start_with_span(side):
        for j in range(heads_here):
            scores = scores_of(side, j, span_buf[0]) + bias_buf[...]
            newest = jnp.max(scores, axis=0, keepdims=True)
            weights = jnp.exp2((scores - newest) * factor)
            m_buf[side, j] = newest
            l_buf[side, j] = jnp.sum(weights, axis=0, keepdims=True)
            acc_buf[side, j] = weighted(span_buf[1], weights)

    def fold(sides, pieces):
        keys, values, bias = [], [], []
        for ref, source in pieces:
            keys.append(ref[0])
            values.append(ref[1])
            at = source * depth + lax.broadcasted_iota(jnp.int32, (depth, slots), 0)
            bias.append(jnp.where(at < length_ref[0], 0.0, NEG_BIG))
        key_rows = keys[0] if len(keys) == 1 else jnp.concatenate(keys, axis=0)
        value_rows = values[0] if len(keys) == 1 else jnp.concatenate(values, axis=0)
        key_bias = bias[0] if len(keys) == 1 else jnp.concatenate(bias, axis=0)
        for side in sides:
            for j in range(heads_here):
                scores = scores_of(side, j, key_rows) + key_bias
                before = m_buf[side, j]
                newest = jnp.maximum(before, jnp.max(scores, axis=0, keepdims=True))
                shrink = jnp.exp2((before - newest) * factor)
                weights = jnp.exp2((scores - newest) * factor)
                m_buf[side, j] = newest
                l_buf[side, j] = l_buf[side, j] * shrink + jnp.sum(weights, axis=0, keepdims=True)
                acc_buf[side, j] = acc_buf[side, j] * shrink + weighted(value_rows, weights)

    loads[0].wait()
    across_rows = jnp.broadcast_to(rows_buf[...].reshape(1, slots), (slots, slots))
    down_rows = across_rows.T
    key_at = lax.broadcasted_iota(jnp.int32, (slots, slots), 0)
    row_at = lax.broadcasted_iota(jnp.int32, (slots, slots), 1)
    allowed = (across_rows == down_rows) & (key_at <= row_at)
    bias_buf[...] = jnp.where(allowed, 0.0, NEG_BIG)
    live_row = across_rows[:1] >= 0

    for load in loads[1:]:
        load.wait()
    start_with_span(0)
    fold((0,), [(own_buf, me)])
    q_send.wait_recv()

    @pl.when(core == 1)
    def _():
        q_send.start()

    start_with_span(1)
    fold((1,), [(own_buf, me)])
    weight_load.start()

    for c in range(n):
        if c not in PRE:

            @on(1, c)
            def _(c=c):
                send_late(c, own_buf)

    def arrive(at):
        @pl.when(core == 0)
        def _():
            relay(at).wait_recv()

        @pl.when(core == 1)
        def _():
            arrival(at).wait_recv()
            relay(at).start()
            for c in range(n):
                if ORDER[c][at] in FORWARD[c]:

                    @pl.when(me == c)
                    def _(c=c):
                        forward(c, ORDER[c][at]).start()

    def sent(blocks, sem):
        part = kv_buf.at[pl.ds(0, blocks)]
        remote(part, part, sem.at[0], recv_sem.at[0], {"tensor": other}).wait_send()

    def source_of(at):
        return sum((me == c).astype(jnp.int32) * ORDER[c][at] for c in range(n))

    for at in range(n - 1):
        if at == n - 2:
            weight_load.wait()
            q_send.wait_send()
            for c in range(n):
                if EARLY[c]:

                    @on(0, c)
                    def _(c=c):
                        sent(len(EARLY[c]), send_sem)

                if LATE[c]:

                    @on(1, c)
                    def _(c=c):
                        sent(len(LATE[c]), send_sem)

        arrive(at)
        fold((0, 1), [(kv_buf.at[at], source_of(at))])

    for side in (0, 1):
        for j in range(heads_here):
            out = jnp.where(live_row, acc_buf[side, j] * (1.0 / l_buf[side, j]), 0.0).T
            place = (core if side == 0 else other) * heads_here + j
            first = pl.multiple_of(place * head_size, head_size)
            head_ref[:, pl.ds(first, head_size)] = out.astype(head_ref.dtype)

    @pl.when(core == 1)
    def _():
        sent(n - 1, relay_send_sem)
        for c in range(n):
            if FORWARD[c]:

                @pl.when(me == c)
                def _(c=c):
                    sent(len(FORWARD[c]), forward_sem)


def project(head_ref, weight_ref, out_hbm, tiles, sems):
    copies = []
    block = tiles.shape[2]
    for at in range(tiles.shape[0]):
        columns = slice(at * block, (at + 1) * block)
        tiles[at] = jnp.dot(
            head_ref[...], weight_ref[:, columns], preferred_element_type=jnp.float32
        ).astype(tiles.dtype)
        copies.append(pltpu.make_async_copy(tiles.at[at], out_hbm.at[:, columns], sems.at[at]))
        copies[-1].start()
    for copy in copies:
        copy.wait()


def body(n, queries, span_kv, prefix_kv, row_candidate, prefix_length, out_weight):
    slots, width = queries.shape
    depth, head_size = prefix_kv.shape[1:]
    heads_here = width // head_size
    anywhere = pl.BlockSpec(memory_space=pltpu.HBM)
    operands = (queries, span_kv, prefix_kv, row_candidate, out_weight)
    row_state = pltpu.VMEM((2, heads_here, 1, slots), jnp.float32)
    both_heads, weight = pl.pallas_call(
        functools.partial(gather_attend, n),
        name="gather_attend",
        out_shape=(
            jax.ShapeDtypeStruct((slots, 2 * width), jnp.bfloat16),
            jax.ShapeDtypeStruct(out_weight.shape, jnp.bfloat16),
        ),
        in_specs=[anywhere] * len(operands) + [pl.BlockSpec(memory_space=pl.ANY)],
        out_specs=[pl.BlockSpec(memory_space=pltpu.VMEM)] * 2,
        scratch_shapes=[
            pltpu.VMEM((2, slots, width), jnp.bfloat16),
            pltpu.VMEM(span_kv.shape, jnp.bfloat16),
            pltpu.VMEM(prefix_kv.shape, jnp.bfloat16),
            pltpu.VMEM(row_candidate.shape, jnp.int32),
            pltpu.SMEM(prefix_length.shape, jnp.int32),
            pltpu.VMEM((n - 1, *prefix_kv.shape), jnp.bfloat16),
            pltpu.VMEM((slots, slots), jnp.float32),
            row_state,
            row_state,
            pltpu.VMEM((2, heads_here, head_size, slots), jnp.float32),
            pltpu.SemaphoreType.DMA((6,)),
            pltpu.SemaphoreType.DMA((2,)),
            pltpu.SemaphoreType.DMA((1,)),
            pltpu.SemaphoreType.DMA((1,)),
            pltpu.SemaphoreType.DMA((n,)),
            pltpu.SemaphoreType.DMA((1,)),
            pltpu.SemaphoreType.DMA((n,)),
        ],
        compiler_params=pltpu.CompilerParams(
            collective_id=0, has_side_effects=True, vmem_limit_bytes=24 << 20
        ),
    )(*[pltpu.with_memory_space_constraint(x, pltpu.HBM) for x in operands], prefix_length)
    features = out_weight.shape[1]
    block = math.gcd(features, 512)
    return pl.pallas_call(
        project,
        name="project",
        out_shape=jax.ShapeDtypeStruct((slots, features), jnp.bfloat16),
        in_specs=[pl.BlockSpec(memory_space=pltpu.VMEM)] * 2,
        out_specs=pl.BlockSpec(memory_space=pltpu.HBM),
        scratch_shapes=[
            pltpu.VMEM((features // block, slots, block), jnp.bfloat16),
            pltpu.SemaphoreType.DMA((features // block,)),
        ],
        compiler_params=pltpu.CompilerParams(vmem_limit_bytes=24 << 20),
    )(both_heads, weight)


def solution(mesh):
    n = mesh.shape["cand"]
    run = functools.partial(body, n) if n == 8 and mesh.shape["tensor"] == 2 else body_large
    return jax.shard_map(
        run,
        mesh=mesh,
        in_specs=(
            P(("groups", "cand"), "tensor"),
            P(None, ("groups", "cand"), None),
            P(None, ("groups", "cand"), None),
            P(("groups", "cand")),
            P("groups"),
            P(None, "tensor"),
        ),
        out_specs=P(("groups", "cand"), "tensor"),
        check_vma=False,
    )
```
